32 devices in a mesh: view: 2 (over core), seq: 16 (over z, y, x).
Axes of the slice: x: 2, y: 2, z: 4, core: 2. Of those that a mesh axis runs over, the one named last changes fastest.
Arguments:
- query: bfloat16 [2, 12288, 2560], P('view', 'seq'), may hold values from -60 to 60
- keys: bfloat16 [2, 12288, 2560], P('view', 'seq'), may hold values from -6 to 6
- values: bfloat16 [2, 12288, 2560], P('view', 'seq'), may hold values from -6 to 6
- block_list: int32 [2, 16, 4], P('view', 'seq'), may hold values from 0 to 5, as said below
- block_count: int32 [2, 16], P('view', 'seq'), may hold values from 1 to 4, as said below
Outputs:
- attended: bfloat16 [2, 12288, 2560], P('view', 'seq')
The draws below stay inside these ranges and needn't reach their ends.
Inputs may be any that keep to these rules, and one draw needn't show every extreme that they name: `block_list`: in each row the first block_count entries are distinct key block indices; later entries are valid indices too. `block_count`: some eye and band uses all 4 entries.
All inputs are finite; a program needn't handle non-finite values.
Results may differ from the reference program's by a relative error of at most 0.0042.
Values may be sent and summed in bfloat16 or wider, within the bound.
A program may use at most 128 MiB of HBM per device.

```python
import jax
import jax.numpy as jnp
from jax import lax

HEADS = 20
HD = 128
TOK_DEV = 768
KBLK = 128
TOKENS = 12288
CELLS = 48
KB = 6
MAXB = 4
N_SEQ = 16


def pair_fields(key):
    feat = HEADS * HD
    query = jax.random.normal(jax.random.fold_in(key, 11), (2, TOKENS, feat), jnp.float32)
    keys = jnp.clip(jax.random.normal(jax.random.fold_in(key, 12), (2, TOKENS, feat), jnp.float32), -6.0, 6.0)
    query = jnp.clip(query, -6.0, 6.0)
    return (query, keys)


def draw_query(key, part):
    return pair_fields(key)[0].astype(jnp.bfloat16)


def draw_keys(key, part):
    return pair_fields(key)[1].astype(jnp.bfloat16)


def list_fields(key):
    rows = 2 * N_SEQ
    subkeys = jax.random.split(jax.random.fold_in(key, 21), rows)
    perms = jax.vmap(lambda sub: jax.random.permutation(sub, KB))(subkeys)
    listed = perms[:, :MAXB].astype(jnp.int32).reshape(2, N_SEQ, MAXB)
    counts = jax.random.randint(jax.random.fold_in(key, 22), (rows,), 1, MAXB + 1, dtype=jnp.int32)
    fullest = jax.random.randint(jax.random.fold_in(key, 23), (), 0, rows, dtype=jnp.int32)
    counts = jnp.where(jnp.arange(rows, dtype=jnp.int32) == fullest, MAXB, counts)
    return (listed, counts.reshape(2, N_SEQ))


def draw_block_list(key, part):
    return list_fields(key)[0]


def draw_block_count(key, part):
    return list_fields(key)[1]


def level_of(stream_key, shape, shards, low, high):
    level, own = 1.0, jax.random.fold_in(stream_key, 6)
    for position, shards_of in shards:
        heights = jnp.exp(jax.random.uniform(jax.random.fold_in(own, position), (shards_of,), jnp.float32, low / len(shards), high / len(shards)))
        level = level * jnp.repeat(heights, shape[position] // shards_of).reshape([-1 if axis == position else 1 for axis in range(len(shape))])
    return level


def gaussian(key, extent, scale, reach, shards=(), kind=jnp.bfloat16):
    entries = jax.random.normal(key, extent, jnp.float32) * scale
    if len(shards) > 0:
        entries = level_of(key, extent, shards, -0.22, 0.18) * entries
    return jnp.clip(entries, min=-reach, max=reach).astype(kind)


def setup_inputs(seed: int = 0) -> dict:
    splits = jax.random.split(jax.random.key(seed), 6)
    return {
        "query": draw_query(jax.random.fold_in(splits[5], 71), 0),
        "keys": draw_keys(jax.random.fold_in(splits[5], 71), 0),
        "values": gaussian(splits[2], (2, TOKENS, HEADS * HD), 1.0, 6.0, ((0, 2), (1, 16))),
        "block_list": draw_block_list(jax.random.fold_in(splits[5], 71), 0),
        "block_count": draw_block_count(jax.random.fold_in(splits[5], 71), 0),
    }


def attend(query, near_k, near_v, far_k, far_v, far_live):
    keys = jnp.concatenate((near_k, far_k), 0)
    vals = jnp.concatenate((near_v, far_v), 0)
    live = jnp.concatenate((jnp.ones((near_k.shape[0],), dtype=bool), far_live), 0)
    scale = HD ** -0.5

    def one_head(head):
        start = (head * HD).astype(jnp.int32)
        qpart = lax.dynamic_slice_in_dim(query, start, HD, 1)
        kpart = lax.dynamic_slice_in_dim(keys, start, HD, 1)
        vpart = lax.dynamic_slice_in_dim(vals, start, HD, 1)
        score = lax.dot_general(qpart, kpart, (((1,), (1,)), ((), ())), preferred_element_type=jnp.float32) * scale
        score = jnp.where(live[None, :], score, -1e30)
        top = jnp.max(score, axis=1, keepdims=True)
        weight = jnp.exp(score - top)
        total = jnp.sum(weight, axis=1, keepdims=True)
        mixed = jnp.dot(weight.astype(jnp.bfloat16), vpart, preferred_element_type=jnp.float32) / total
        return mixed.astype(jnp.bfloat16)

    outs = lax.map(one_head, jnp.arange(HEADS, dtype=jnp.int32))
    return jnp.transpose(outs, (1, 0, 2)).reshape(query.shape[0], HEADS * HD)


def block_mask(listed, count, blocks, width):
    slots = jnp.arange(listed.shape[0], dtype=jnp.int32)
    hits = (listed[:, None] == jnp.arange(blocks, dtype=jnp.int32)[None, :]) & (slots < count)[:, None]
    return jnp.repeat(jnp.any(hits, axis=0), width, total_repeat_length=blocks * width)


def reference(query, keys, values, block_list, block_count):
    feat = HEADS * HD

    def to_bands(x):
        return x.reshape(2, N_SEQ, N_SEQ, CELLS, feat).transpose(0, 2, 1, 3, 4).reshape(2 * N_SEQ, TOK_DEV, feat)

    band_q = to_bands(query)
    band_k = to_bands(keys)
    band_v = to_bands(values)
    lists = block_list.reshape(2 * N_SEQ, MAXB)
    counts = block_count.reshape(2 * N_SEQ)

    def one_band(index):
        other = (index + N_SEQ) % (2 * N_SEQ)
        live = block_mask(lists[index], counts[index], KB, KBLK)
        return attend(band_q[index], band_k[index], band_v[index], band_k[other], band_v[other], live)

    mixed = lax.map(one_band, jnp.arange(2 * N_SEQ, dtype=jnp.int32))
    return mixed.reshape(2, N_SEQ, N_SEQ, CELLS, feat).transpose(0, 2, 1, 3, 4).reshape(2, TOKENS, feat)
```

```python
import functools

import jax
import jax.numpy as jnp
from jax import lax
from jax.experimental import pallas as pl
from jax.experimental.pallas import tpu as pltpu
from jax.sharding import PartitionSpec as P

HD = 128
KBLK = 128
GROUP_HEADS = 4
ROWS = 256
MESH = pl.DeviceIdType.MESH


def block_mask(listed, count, blocks, width):
    slots = jnp.arange(listed.shape[0], dtype=jnp.int32)
    hits = (listed[:, None] == jnp.arange(blocks, dtype=jnp.int32)[None, :]) & (slots < count)[
        :, None
    ]
    return jnp.repeat(jnp.any(hits, axis=0), width, total_repeat_length=blocks * width)


def attend_tile(q, near_k, near_v, far_k, far_v, bias):
    scale = HD**-0.5
    dims = (((1,), (1,)), ((), ()))
    near = lax.dot_general(q, near_k, dims, preferred_element_type=jnp.float32)
    far = lax.dot_general(q, far_k, dims, preferred_element_type=jnp.float32) + bias
    top = jnp.maximum(
        jnp.max(near, axis=1, keepdims=True), jnp.max(far, axis=1, keepdims=True)
    )
    near_w = jnp.exp((near - top) * scale)
    far_w = jnp.exp((far - top) * scale)
    total = jnp.sum(near_w, axis=1, keepdims=True) + jnp.sum(far_w, axis=1, keepdims=True)
    mixed = jnp.dot(near_w.astype(jnp.bfloat16), near_v, preferred_element_type=jnp.float32)
    mixed += jnp.dot(far_w.astype(jnp.bfloat16), far_v, preferred_element_type=jnp.float32)
    return (mixed / total).astype(jnp.bfloat16)


def wait_for(ref, sem):
    pltpu.make_async_copy(ref, ref, sem).wait()


def kernel(n, cells, q, k, v, bias, out, qb, kb, vb, fk, fv, ob,
           send, recv, far_send, far_recv, out_send, out_recv):
    me = lax.axis_index("seq")
    view = lax.axis_index("view")
    rows, feat = qb.shape
    width = GROUP_HEADS * HD if feat % (GROUP_HEADS * HD) == 0 else HD
    groups = feat // width
    tile = ROWS if rows % ROWS == 0 else rows

    def span(d):
        return pl.ds(pl.multiple_of(d * cells, cells), cells)

    def peer(i):
        return lax.rem(me + i, n)

    barrier = pltpu.get_barrier_semaphore()

    @pl.loop(1, n)
    def _(i):
        pl.semaphore_signal(barrier, inc=1, device_id=(view, peer(i)), device_id_type=MESH)

    pl.semaphore_signal(barrier, inc=1, device_id=(1 - view, me), device_id_type=MESH)
    pl.semaphore_wait(barrier, n)

    moved = ((q, qb), (k, kb), (v, vb))
    for g in range(groups):
        cols = pl.ds(g * width, width)
        for a, (src, dst) in enumerate(moved):
            pltpu.make_async_copy(
                src.at[span(me), cols], dst.at[span(me), cols], recv.at[g, a]
            ).start()

        @pl.loop(1, n)
        def _(i):
            d = peer(i)
            for a, (src, dst) in enumerate(moved):
                pltpu.make_async_remote_copy(
                    src_ref=src.at[span(d), cols],
                    dst_ref=dst.at[span(me), cols],
                    send_sem=send.at[g, a],
                    recv_sem=recv.at[g, a],
                    device_id=(view, d),
                    device_id_type=MESH,
                ).start()

    for g in range(groups):
        cols = pl.ds(g * width, width)
        far = []
        for a, (near, other) in enumerate(((kb, fk), (vb, fv))):
            wait_for(near.at[:, cols], recv.at[g, a + 1])
            copy = pltpu.make_async_remote_copy(
                src_ref=near.at[:, cols],
                dst_ref=other.at[:, cols],
                send_sem=far_send.at[g, a],
                recv_sem=far_recv.at[g, a],
                device_id=(1 - view, me),
                device_id_type=MESH,
            )
            copy.start()
            far.append(copy)
        wait_for(qb.at[:, cols], recv.at[g, 0])
        for copy in far:
            copy.wait()

        @pl.loop(0, width // HD)
        def _(h):
            col = pl.ds(pl.multiple_of(g * width + h * HD, HD), HD)
            near_k, near_v, far_k, far_v = kb[:, col], vb[:, col], fk[:, col], fv[:, col]
            for r in range(rows // tile):
                part = pl.ds(r * tile, tile)
                ob[part, col] = attend_tile(
                    qb[part, col], near_k, near_v, far_k, far_v, bias[...]
                )

        pltpu.make_async_copy(ob.at[span(me), cols], out.at[span(me), cols], out_recv).start()

        @pl.loop(1, n)
        def _(i):
            d = peer(i)
            pltpu.make_async_remote_copy(
                src_ref=ob.at[span(d), cols],
                dst_ref=out.at[span(me), cols],
                send_sem=out_send,
                recv_sem=out_recv,
                device_id=(view, d),
                device_id_type=MESH,
            ).start()

    sent = pl.ds(0, (n - 1) * cells)
    for g in range(groups):
        cols = pl.ds(g * width, width)
        for a, (src, _) in enumerate(moved):
            wait_for(src.at[sent, cols], send.at[g, a])
    wait_for(ob.at[sent, :], out_send)
    wait_for(out, out_recv)


def by_kernel(query, keys, values, live):
    n = lax.axis_size("seq")
    rows, feat = query.shape
    cells = rows // n
    bias = jnp.where(live, 0.0, -1e30).astype(jnp.float32)[None, :]
    width = GROUP_HEADS * HD if feat % (GROUP_HEADS * HD) == 0 else HD
    groups = feat // width
    anywhere = pl.BlockSpec(memory_space=pl.ANY)
    sems = pltpu.SemaphoreType.DMA
    return pl.pallas_call(
        functools.partial(kernel, n, cells),
        out_shape=jax.ShapeDtypeStruct((rows, feat), jnp.bfloat16),
        in_specs=[anywhere, anywhere, anywhere, pl.BlockSpec(memory_space=pltpu.VMEM)],
        out_specs=anywhere,
        scratch_shapes=[pltpu.VMEM((rows, feat), jnp.bfloat16)] * 6
        + [
            sems((groups, 3)),
            sems((groups, 3)),
            sems((groups, 2)),
            sems((groups, 2)),
            sems,
            sems,
        ],
        compiler_params=pltpu.CompilerParams(
            collective_id=0, has_side_effects=True, vmem_limit_bytes=56 * 1024 * 1024
        ),
    )(query, keys, values, bias)


def by_collectives(query, keys, values, live):
    n = lax.axis_size("seq")
    rows, feat = query.shape

    def swap(x):
        x = x.reshape(n, rows // n, feat)
        return lax.all_to_all(x, "seq", split_axis=0, concat_axis=0, tiled=True).reshape(rows, feat)

    def partner(x):
        return lax.ppermute(x, "view", [(0, 1), (1, 0)])

    band_k, band_v = swap(keys), swap(values)
    far_k, far_v = partner(band_k), partner(band_v)
    band_q = swap(query)
    bias = jnp.where(live, 0.0, -1e30).astype(jnp.float32)[None, :]

    def one_head(head):
        parts = [
            lax.dynamic_slice_in_dim(x, head * HD, HD, 1)
            for x in (band_q, band_k, band_v, far_k, far_v)
        ]
        return attend_tile(*parts, bias)

    outs = lax.map(one_head, jnp.arange(feat // HD, dtype=jnp.int32))
    return swap(jnp.transpose(outs, (1, 0, 2)).reshape(rows, feat))


def per_device(query, keys, values, block_list, block_count):
    rows = query.shape[1]
    blocks = rows // KBLK
    live = block_mask(block_list[0, 0], block_count[0, 0], blocks, KBLK)
    aligned = rows // lax.axis_size("seq") % 16 == 0
    run = by_kernel if aligned else by_collectives
    return run(query[0], keys[0], values[0], live)[None]


def solution(mesh):
    in_specs = (
        P("view", "seq", None),
        P("view", "seq", None),
        P("view", "seq", None),
        P("view", "seq", None),
        P("view", "seq"),
    )
    return jax.shard_map(
        per_device, mesh=mesh, in_specs=in_specs, out_specs=P("view", "seq", None), check_vma=False
    )
```

```python
import functools

import jax
import jax.numpy as jnp
from jax import lax
from jax.experimental import pallas as pl
from jax.experimental.pallas import tpu as pltpu
from jax.sharding import PartitionSpec as P

HD = 128
KBLK = 128
GROUP_HEADS = 2
LAST_HEADS = (1, 1)
ROWS = 256
MESH = pl.DeviceIdType.MESH


def block_mask(listed, count, blocks, width):
    slots = jnp.arange(listed.shape[0], dtype=jnp.int32)
    hits = (listed[:, None] == jnp.arange(blocks, dtype=jnp.int32)[None, :]) & (slots < count)[
        :, None
    ]
    return jnp.repeat(jnp.any(hits, axis=0), width, total_repeat_length=blocks * width)


def attend_tile(q, near_k, near_v, far_k, far_v, bias):
    scale = HD**-0.5
    dims = (((1,), (1,)), ((), ()))
    near = lax.dot_general(q, near_k, dims, preferred_element_type=jnp.float32)
    far = lax.dot_general(q, far_k, dims, preferred_element_type=jnp.float32) + bias
    top = jnp.maximum(
        jnp.max(near, axis=1, keepdims=True), jnp.max(far, axis=1, keepdims=True)
    )
    near_w = jnp.exp((near - top) * scale)
    far_w = jnp.exp((far - top) * scale)
    total = jnp.sum(near_w, axis=1, keepdims=True) + jnp.sum(far_w, axis=1, keepdims=True)
    mixed = jnp.dot(near_w.astype(jnp.bfloat16), near_v, preferred_element_type=jnp.float32)
    mixed += jnp.dot(far_w.astype(jnp.bfloat16), far_v, preferred_element_type=jnp.float32)
    return (mixed / total).astype(jnp.bfloat16)


def head_groups(heads):
    tail = LAST_HEADS if heads > sum(LAST_HEADS) else ()
    left = heads - sum(tail)
    sizes = [min(GROUP_HEADS, left - done) for done in range(0, left, GROUP_HEADS)]
    groups, start = [], 0
    for size in (*sizes, *tail):
        groups.append((start, size))
        start += size
    return groups


def wait_for(ref, sem):
    pltpu.make_async_copy(ref, ref, sem).wait()


def kernel(n, cells, q, k, v, listed, count, out, qb, kb, vb, fk, fv, ob, bias,
           send, recv, far_send, far_recv, out_send, out_recv):
    me = lax.axis_index("seq")
    view = lax.axis_index("view")
    rows, feat = qb.shape
    groups = head_groups(feat // HD)
    stride = n // 2 - 1 if n % 4 == 0 and n > 4 else 1
    tile = ROWS if rows % ROWS == 0 else rows

    def span(d):
        return pl.ds(pl.multiple_of(d * cells, cells), cells)

    def peer(i):
        return lax.rem(me + i * stride, n)

    barrier = pltpu.get_barrier_semaphore()

    @pl.loop(1, n)
    def _(i):
        pl.semaphore_signal(barrier, inc=1, device_id=(view, peer(i)), device_id_type=MESH)

    pl.semaphore_signal(barrier, inc=1, device_id=(1 - view, me), device_id_type=MESH)
    pl.semaphore_wait(barrier, n)

    moved = ((q, qb), (k, kb), (v, vb))
    for g, (first, size) in enumerate(groups):
        cols = pl.ds(first * HD, size * HD)
        for a, (src, dst) in enumerate(moved):
            pltpu.make_async_copy(
                src.at[span(me), cols], dst.at[span(me), cols], recv.at[g, a]
            ).start()

        @pl.loop(1, n)
        def _(i):
            d = peer(i)
            for a, (src, dst) in enumerate(moved):
                pltpu.make_async_remote_copy(
                    src_ref=src.at[span(d), cols],
                    dst_ref=dst.at[span(me), cols],
                    send_sem=send.at[g, a],
                    recv_sem=recv.at[g, a],
                    device_id=(view, d),
                    device_id_type=MESH,
                ).start()

    token = lax.broadcasted_iota(jnp.int32, (1, rows), 1)
    live = token < 0
    for m in range(listed.shape[0]):
        low = jnp.where(m < count[0], listed[m], -1) * KBLK
        live |= (token >= low) & (token < low + KBLK)
    bias[...] = jnp.where(live, 0.0, -1e30)

    for g, (first, size) in enumerate(groups):
        cols = pl.ds(first * HD, size * HD)
        far = []
        for a, (near, other) in enumerate(((kb, fk), (vb, fv))):
            wait_for(near.at[:, cols], recv.at[g, a + 1])
            copy = pltpu.make_async_remote_copy(
                src_ref=near.at[:, cols],
                dst_ref=other.at[:, cols],
                send_sem=far_send.at[g, a],
                recv_sem=far_recv.at[g, a],
                device_id=(1 - view, me),
                device_id_type=MESH,
            )
            copy.start()
            far.append(copy)
        wait_for(qb.at[:, cols], recv.at[g, 0])
        for copy in far:
            copy.wait()

        @pl.loop(0, size)
        def _(h):
            col = pl.ds(pl.multiple_of((first + h) * HD, HD), HD)
            near_k, near_v, far_k, far_v = kb[:, col], vb[:, col], fk[:, col], fv[:, col]
            for r in range(rows // tile):
                part = pl.ds(r * tile, tile)
                ob[part, col] = attend_tile(
                    qb[part, col], near_k, near_v, far_k, far_v, bias[...]
                )

        pltpu.make_async_copy(ob.at[span(me), cols], out.at[span(me), cols], out_recv).start()

        @pl.loop(1, n)
        def _(i):
            d = peer(i)
            pltpu.make_async_remote_copy(
                src_ref=ob.at[span(d), cols],
                dst_ref=out.at[span(me), cols],
                send_sem=out_send,
                recv_sem=out_recv,
                device_id=(view, d),
                device_id_type=MESH,
            ).start()

    sent = pl.ds(0, (n - 1) * cells)
    for g, (first, size) in enumerate(groups):
        cols = pl.ds(first * HD, size * HD)
        for a, (src, _) in enumerate(moved):
            wait_for(src.at[sent, cols], send.at[g, a])
    wait_for(ob.at[sent, :], out_send)
    wait_for(out, out_recv)


def by_kernel(query, keys, values, listed, count):
    n = lax.axis_size("seq")
    rows, feat = query.shape
    cells = rows // n
    groups = len(head_groups(feat // HD))
    anywhere = pl.BlockSpec(memory_space=pl.ANY)
    sems = pltpu.SemaphoreType.DMA
    return pl.pallas_call(
        functools.partial(kernel, n, cells),
        out_shape=jax.ShapeDtypeStruct((rows, feat), jnp.bfloat16),
        in_specs=[anywhere] * 3 + [pl.BlockSpec(memory_space=pltpu.SMEM)] * 2,
        out_specs=anywhere,
        scratch_shapes=[pltpu.VMEM((rows, feat), jnp.bfloat16)] * 6
        + [
            pltpu.VMEM((1, rows), jnp.float32),
            sems((groups, 3)),
            sems((groups, 3)),
            sems((groups, 2)),
            sems((groups, 2)),
            sems,
            sems,
        ],
        compiler_params=pltpu.CompilerParams(
            collective_id=0, has_side_effects=True, vmem_limit_bytes=56 * 1024 * 1024
        ),
    )(query, keys, values, listed, count)


def by_collectives(query, keys, values, listed, count):
    n = lax.axis_size("seq")
    rows, feat = query.shape
    live = block_mask(listed, count[0], rows // KBLK, KBLK)

    def swap(x):
        x = x.reshape(n, rows // n, feat)
        return lax.all_to_all(x, "seq", split_axis=0, concat_axis=0, tiled=True).reshape(rows, feat)

    def partner(x):
        return lax.ppermute(x, "view", [(0, 1), (1, 0)])

    band_k, band_v = swap(keys), swap(values)
    far_k, far_v = partner(band_k), partner(band_v)
    band_q = swap(query)
    bias = jnp.where(live, 0.0, -1e30).astype(jnp.float32)[None, :]

    def one_head(head):
        parts = [
            lax.dynamic_slice_in_dim(x, head * HD, HD, 1)
            for x in (band_q, band_k, band_v, far_k, far_v)
        ]
        return attend_tile(*parts, bias)

    outs = lax.map(one_head, jnp.arange(feat // HD, dtype=jnp.int32))
    return swap(jnp.transpose(outs, (1, 0, 2)).reshape(rows, feat))


def per_device(query, keys, values, block_list, block_count):
    aligned = query.shape[1] // lax.axis_size("seq") % 16 == 0
    run = by_kernel if aligned else by_collectives
    return run(query[0], keys[0], values[0], block_list[0, 0], block_count[0])[None]


def solution(mesh):
    in_specs = (
        P("view", "seq", None),
        P("view", "seq", None),
        P("view", "seq", None),
        P("view", "seq", None),
        P("view", "seq"),
    )
    return jax.shard_map(
        per_device, mesh=mesh, in_specs=in_specs, out_specs=P("view", "seq", None), check_vma=False
    )
```

```python
import functools

import jax
import jax.numpy as jnp
from jax import lax
from jax.experimental import pallas as pl
from jax.experimental.pallas import tpu as pltpu
from jax.sharding import PartitionSpec as P

HD = 128
KBLK = 128
GROUP_HEADS = 2
LAST_HEADS = (1, 1)
ROWS = 256
MESH = pl.DeviceIdType.MESH


def block_mask(listed, count, blocks, width):
    slots = jnp.arange(listed.shape[0], dtype=jnp.int32)
    hits = (listed[:, None] == jnp.arange(blocks, dtype=jnp.int32)[None, :]) & (slots < count)[
        :, None
    ]
    return jnp.repeat(jnp.any(hits, axis=0), width, total_repeat_length=blocks * width)


def attend_tile(q, near_k, near_v, far_k, far_v, bias):
    scale = HD**-0.5
    dims = (((1,), (1,)), ((), ()))
    near = lax.dot_general(q, near_k, dims, preferred_element_type=jnp.float32)
    far = lax.dot_general(q, far_k, dims, preferred_element_type=jnp.float32) + bias
    top = jnp.maximum(
        jnp.max(near, axis=1, keepdims=True), jnp.max(far, axis=1, keepdims=True)
    )
    near_w = jnp.exp((near - top) * scale)
    far_w = jnp.exp((far - top) * scale)
    total = jnp.sum(near_w, axis=1, keepdims=True) + jnp.sum(far_w, axis=1, keepdims=True)
    mixed = jnp.dot(near_w.astype(jnp.bfloat16), near_v, preferred_element_type=jnp.float32)
    mixed += jnp.dot(far_w.astype(jnp.bfloat16), far_v, preferred_element_type=jnp.float32)
    return (mixed / total).astype(jnp.bfloat16)


def head_groups(heads):
    tail = LAST_HEADS if heads > sum(LAST_HEADS) else ()
    left = heads - sum(tail)
    sizes = [min(GROUP_HEADS, left - done) for done in range(0, left, GROUP_HEADS)]
    groups, start = [], 0
    for size in (*sizes, *tail):
        groups.append((start, size))
        start += size
    return groups


def wait_for(ref, sem):
    pltpu.make_async_copy(ref, ref, sem).wait()


def kernel(n, cells, q, k, v, listed, count, out, qb, kb, vb, fk, fv, ob, bias,
           send, recv, far_send, far_recv, out_send, out_recv):
    me = lax.axis_index("seq")
    view = lax.axis_index("view")
    rows, feat = qb.shape
    groups = head_groups(feat // HD)
    stride = n // 2 - 1 if n % 4 == 0 and n > 4 else 1
    tile = ROWS if rows % ROWS == 0 else rows

    def span(d):
        return pl.ds(pl.multiple_of(d * cells, cells), cells)

    def peer(i):
        return lax.rem(me + i * stride, n)

    barrier = pltpu.get_barrier_semaphore()

    @pl.loop(1, n)
    def _(i):
        pl.semaphore_signal(barrier, inc=1, device_id=(view, peer(i)), device_id_type=MESH)

    pl.semaphore_signal(barrier, inc=1, device_id=(1 - view, me), device_id_type=MESH)
    pl.semaphore_wait(barrier, n)

    moved = ((k, kb), (v, vb), (q, qb))
    for g, (first, size) in enumerate(groups):
        cols = pl.ds(first * HD, size * HD)
        for a, (src, dst) in enumerate(moved):
            pltpu.make_async_copy(
                src.at[span(me), cols], dst.at[span(me), cols], recv.at[g, a]
            ).start()

        @pl.loop(1, n)
        def _(i):
            d = peer(i)
            for a, (src, dst) in enumerate(moved):
                pltpu.make_async_remote_copy(
                    src_ref=src.at[span(d), cols],
                    dst_ref=dst.at[span(me), cols],
                    send_sem=send.at[g, a],
                    recv_sem=recv.at[g, a],
                    device_id=(view, d),
                    device_id_type=MESH,
                ).start()

    token = lax.broadcasted_iota(jnp.int32, (1, rows), 1)
    live = token < 0
    for m in range(listed.shape[0]):
        low = jnp.where(m < count[0], listed[m], -1) * KBLK
        live |= (token >= low) & (token < low + KBLK)
    bias[...] = jnp.where(live, 0.0, -1e30)

    for g, (first, size) in enumerate(groups):
        cols = pl.ds(first * HD, size * HD)
        far = []
        for a, (near, other) in enumerate(((kb, fk), (vb, fv))):
            wait_for(near.at[:, cols], recv.at[g, a])
            copy = pltpu.make_async_remote_copy(
                src_ref=near.at[:, cols],
                dst_ref=other.at[:, cols],
                send_sem=far_send.at[g, a],
                recv_sem=far_recv.at[g, a],
                device_id=(1 - view, me),
                device_id_type=MESH,
            )
            copy.start()
            far.append(copy)
        wait_for(qb.at[:, cols], recv.at[g, 2])
        for copy in far:
            copy.wait()

        @pl.loop(0, size)
        def _(h):
            col = pl.ds(pl.multiple_of((first + h) * HD, HD), HD)
            near_k, near_v, far_k, far_v = kb[:, col], vb[:, col], fk[:, col], fv[:, col]
            for r in range(rows // tile):
                part = pl.ds(r * tile, tile)
                ob[part, col] = attend_tile(
                    qb[part, col], near_k, near_v, far_k, far_v, bias[...]
                )

        pltpu.make_async_copy(ob.at[span(me), cols], out.at[span(me), cols], out_recv).start()

        @pl.loop(1, n)
        def _(i):
            d = peer(i)
            pltpu.make_async_remote_copy(
                src_ref=ob.at[span(d), cols],
                dst_ref=out.at[span(me), cols],
                send_sem=out_send,
                recv_sem=out_recv,
                device_id=(view, d),
                device_id_type=MESH,
            ).start()

    sent = pl.ds(0, (n - 1) * cells)
    for g, (first, size) in enumerate(groups):
        cols = pl.ds(first * HD, size * HD)
        for a, (src, _) in enumerate(moved):
            wait_for(src.at[sent, cols], send.at[g, a])
    wait_for(ob.at[sent, :], out_send)
    wait_for(out, out_recv)


def by_kernel(query, keys, values, listed, count):
    n = lax.axis_size("seq")
    rows, feat = query.shape
    cells = rows // n
    groups = len(head_groups(feat // HD))
    anywhere = pl.BlockSpec(memory_space=pl.ANY)
    sems = pltpu.SemaphoreType.DMA
    return pl.pallas_call(
        functools.partial(kernel, n, cells),
        out_shape=jax.ShapeDtypeStruct((rows, feat), jnp.bfloat16),
        in_specs=[anywhere] * 3 + [pl.BlockSpec(memory_space=pltpu.SMEM)] * 2,
        out_specs=anywhere,
        scratch_shapes=[pltpu.VMEM((rows, feat), jnp.bfloat16)] * 6
        + [
            pltpu.VMEM((1, rows), jnp.float32),
            sems((groups, 3)),
            sems((groups, 3)),
            sems((groups, 2)),
            sems((groups, 2)),
            sems,
            sems,
        ],
        compiler_params=pltpu.CompilerParams(
            collective_id=0, has_side_effects=True, vmem_limit_bytes=56 * 1024 * 1024
        ),
    )(query, keys, values, listed, count)


def by_collectives(query, keys, values, listed, count):
    n = lax.axis_size("seq")
    rows, feat = query.shape
    live = block_mask(listed, count[0], rows // KBLK, KBLK)

    def swap(x):
        x = x.reshape(n, rows // n, feat)
        return lax.all_to_all(x, "seq", split_axis=0, concat_axis=0, tiled=True).reshape(rows, feat)

    def partner(x):
        return lax.ppermute(x, "view", [(0, 1), (1, 0)])

    band_k, band_v = swap(keys), swap(values)
    far_k, far_v = partner(band_k), partner(band_v)
    band_q = swap(query)
    bias = jnp.where(live, 0.0, -1e30).astype(jnp.float32)[None, :]

    def one_head(head):
        parts = [
            lax.dynamic_slice_in_dim(x, head * HD, HD, 1)
            for x in (band_q, band_k, band_v, far_k, far_v)
        ]
        return attend_tile(*parts, bias)

    outs = lax.map(one_head, jnp.arange(feat // HD, dtype=jnp.int32))
    return swap(jnp.transpose(outs, (1, 0, 2)).reshape(rows, feat))


def per_device(query, keys, values, block_list, block_count):
    aligned = query.shape[1] // lax.axis_size("seq") % 16 == 0
    run = by_kernel if aligned else by_collectives
    return run(query[0], keys[0], values[0], block_list[0, 0], block_count[0])[None]


def solution(mesh):
    in_specs = (
        P("view", "seq", None),
        P("view", "seq", None),
        P("view", "seq", None),
        P("view", "seq", None),
        P("view", "seq"),
    )
    return jax.shard_map(
        per_device, mesh=mesh, in_specs=in_specs, out_specs=P("view", "seq", None), check_vma=False
    )
```
